256 devices in a mesh: cell: 32 (over z, y_hi, core), period: 8 (over x, y_lo).
Axes of the slice: x: 4, y: 4 (y_hi: 2, y_lo: 2; y = y_hi * 2 + y_lo), z: 8, core: 2. Of those that a mesh axis runs over, the one named last changes fastest.
Arguments:
- footprints: float32 [32, 16, 32768], P(None, 'period', 'cell'), may hold values from -16 to 16
- cell_coords: int32 [2, 32768], P(None, 'cell'), may hold values from 0 to 255, as said below
- obs_period: int32 [32], replicated, may hold values from 0 to 15
- temporal_cov: float32 [16, 16], replicated, may hold values from -1.5 to 1.5
Outputs:
- hq_field: float32 [32, 16, 32768], P(None, 'period', 'cell')
- hqh_gram: float32 [32, 32], replicated
The draws below stay inside these ranges and needn't reach their ends.
Inputs may be any that keep to these rules, and one draw needn't show every extreme that they name: `cell_coords`: cells sit at distinct grid points that together fill the rectangle of first coordinates 0 to 255 and second coordinates 0 to 127.
All inputs are finite; a program needn't handle non-finite values.
Results may differ from the reference program's by a relative error of at most 0.0003.
Values sent between devices are 32-bit elements; how exact they have to be, the bound alone decides.
No kernel may reach another device: no remote copies, remote signals or barrier semaphores. Data moves between devices by JAX's collectives and lax.ppermute only.
A program may use at most 64 MiB of HBM per device.

```python
import jax
import jax.numpy as jnp
from jax import lax

OBS = 32
PERIODS = 16
CELLS = 32768


def grid_order(key):
    return jax.random.permutation(jax.random.fold_in(key, 11), CELLS).astype(jnp.int32)


def draw_cell_coords(key, part):
    places = grid_order(key)
    return jnp.stack([places % 256, places // 256]).astype(jnp.int32)


def draw_footprints(key, part):
    places = grid_order(key)
    noise_key = jax.random.fold_in(key, 23)
    values = 0.5 * jax.random.truncated_normal(noise_key, -3.0, 3.0, (OBS, PERIODS, CELLS), jnp.float32)
    column = jnp.arange(CELLS, dtype=jnp.int32) % 256
    inside = ((column >= 12) & (column < 244)).astype(jnp.float32)
    values = values * inside[None, None, :]
    near = jnp.roll(values, 6, axis=2) + jnp.roll(values, -6, axis=2)
    far = jnp.roll(values, 12, axis=2) + jnp.roll(values, -12, axis=2)
    field = 6.0 * values - 4.0 * near + far
    field = jnp.clip(field, -16.0, 16.0)
    return jnp.take(field, places, axis=2).astype(jnp.float32)


def touch_ends(entries, key, least, largest):
    extent = entries.shape
    index_at = [jax.random.randint(jax.random.fold_in(key, axis), (), 0, extent[axis]) for axis in range(len(extent))]
    entries = entries.at[tuple(index_at)].set(least)
    longest = extent.index(max(extent))
    index_at[longest] = (index_at[longest] + 1) % extent[longest]
    return entries.at[tuple(index_at)].set(largest)


def centred(key, extent, deviation, limit, held_as=jnp.bfloat16):
    return jnp.clip(deviation * jax.random.normal(key, extent, jnp.float32), -limit, limit).astype(held_as)


def setup_inputs(seed: int = 0) -> dict:
    seeds = jax.random.split(jax.random.key(seed), 5)
    footprints = draw_footprints(jax.random.fold_in(seeds[4], 71), 0)
    cell_coords = draw_cell_coords(jax.random.fold_in(seeds[4], 71), 0)
    obs_period = touch_ends(jax.random.randint(seeds[2], (OBS,), 0, PERIODS), jax.random.fold_in(seeds[2], 1), 0, PERIODS - 1).astype(jnp.int32)
    temporal_cov = centred(seeds[3], (PERIODS, PERIODS), PERIODS ** -0.5, 1.5, jnp.float32)
    return {"footprints": footprints, "cell_coords": cell_coords, "obs_period": obs_period, "temporal_cov": temporal_cov}


LENGTH_SCALE = 48.0

def covariance_tile(first_xy, second_xy):
    delta_x = first_xy[0][:, None] - second_xy[0][None, :]
    delta_y = first_xy[1][:, None] - second_xy[1][None, :]
    return jnp.exp(-jnp.sqrt(delta_x * delta_x + delta_y * delta_y) / LENGTH_SCALE)

def reference(footprints, cell_coords, obs_period, temporal_cov):
    places = cell_coords.astype(jnp.float32)
    period_ids = jnp.arange(PERIODS, dtype=jnp.int32)
    keep = (period_ids[None, :, None] <= obs_period[:, None, None]).astype(jnp.float32)
    masked = footprints * keep
    flat_rows = masked.reshape(OBS * PERIODS, CELLS)
    block_width = min(512, CELLS)
    count_blocks = CELLS // block_width

    def column_block(block_index):
        column_places = lax.dynamic_slice_in_dim(places, (block_index * block_width).astype(jnp.int32), block_width, 1)
        return jnp.dot(flat_rows, covariance_tile(places, column_places), precision=lax.Precision.HIGHEST, preferred_element_type=jnp.float32)
    spatial = lax.map(column_block, jnp.arange(count_blocks, dtype=jnp.int32))
    spatial = jnp.transpose(spatial, (1, 0, 2)).reshape(OBS, PERIODS, CELLS)
    hq_field = jnp.einsum('tu,nuj->ntj', temporal_cov, spatial, precision=lax.Precision.HIGHEST)
    hqh_gram = jnp.einsum('ntj,mtj->nm', hq_field, masked, precision=lax.Precision.HIGHEST)
    return (hq_field, hqh_gram)
```

```python
import jax
import jax.numpy as jnp
import numpy as np
from jax import lax
from jax.experimental import pallas as pl
from jax.experimental.pallas import tpu as pltpu
from jax.sharding import Mesh, PartitionSpec as P
LENGTH_SCALE=48.0
W,H=256,128
def real_basis(n, keep):
    pos=np.arange(keep)[None,:]; rows=[]
    k=np.arange(n)[:,None]
    freq=np.where(k<=n//2,k,n-k)
    ang=2*np.pi*((freq*pos)%n)/n
    b=np.where(k<=n//2,np.cos(ang),np.sin(ang))*np.sqrt(2.0/n)
    b[0]/=np.sqrt(2.0); b[n//2]/=np.sqrt(2.0)
    return b, np.where(np.arange(n)<=n//2,np.arange(n),n-np.arange(n))
def constants():
    bx,fx=real_basis(2*W,W); by,fy=real_basis(2*H,H)
    dx=np.minimum(np.arange(2*W),2*W-np.arange(2*W)); dy=np.minimum(np.arange(2*H),2*H-np.arange(2*H))
    cov=np.exp(-np.sqrt(dy[:,None]**2.0+dx[None,:]**2.0)/LENGTH_SCALE)
    lam=np.real(np.fft.fft2(cov))
    lam=lam[fy][:,fx]
    return bx,by,lam
HI=lax.Precision.HIGHEST
NT=(((1,),(1,)),((),()))
def spatial_kernel(inp_ref,bxt_ref,bxi_ref,by_ref,byt_ref,lam_ref,out_ref,acc_ref,tab_ref):
    n_lists=inp_ref.shape[0]; L=inp_ref.shape[2]
    acc_ref[...]=jnp.zeros_like(acc_ref)
    def onehot(col,count):
        ids=lax.broadcasted_iota(jnp.int32,(count,L),0).astype(jnp.float32).astype(jnp.bfloat16)
        return ids==col.astype(jnp.bfloat16)
    def place(c,_):
        blk=inp_ref[c]
        xs=blk[2:3,:]; ys=blk[3:4,:]
        my=onehot(ys,H); mx=onehot(xs,W)
        parts=[]
        for r in range(2):
            f=blk[r:r+1,:]
            hi=f.astype(jnp.bfloat16); lo=(f-hi.astype(jnp.float32)).astype(jnp.bfloat16)
            lo2=(f-hi.astype(jnp.float32)-lo.astype(jnp.float32)).astype(jnp.bfloat16)
            for p in (hi,lo,lo2):
                parts.append(jnp.where(my,p,jnp.bfloat16(0)))
        a=jnp.concatenate(parts,0)
        b=jnp.where(mx,jnp.bfloat16(1),jnp.bfloat16(0))
        acc_ref[...]+=lax.dot_general(a,b,NT,preferred_element_type=jnp.float32)
        return 0
    lax.fori_loop(0,n_lists,place,0,unroll=4)
    for r in range(2):
        g=acc_ref[384*r:384*r+128,:]+(acc_ref[384*r+128:384*r+256,:]+acc_ref[384*r+256:384*r+384,:])
        u=jnp.dot(g,bxt_ref[...],precision=HI,preferred_element_type=jnp.float32)
        z=jnp.dot(by_ref[...],u,precision=HI,preferred_element_type=jnp.float32)
        z=z*lam_ref[...]
        v=jnp.dot(byt_ref[...],z,precision=HI,preferred_element_type=jnp.float32)
        ht=lax.dot_general(bxi_ref[...],v,NT,precision=HI,preferred_element_type=jnp.float32)
        hi=ht.astype(jnp.bfloat16); lo=(ht-hi.astype(jnp.float32)).astype(jnp.bfloat16)
        for xm in range(4):
            tab_ref[64*r:64*r+64,128*xm:128*xm+128]=hi[64*xm:64*xm+64,:]
            tab_ref[64*r:64*r+64,512+128*xm:512+128*xm+128]=lo[64*xm:64*xm+64,:]
    def pick(c,_):
        blk=inp_ref[c]
        xs=blk[2:3,:]; ys=blk[3:4,:]
        xm=jnp.floor(xs*(1.0/64)); xq=xs-64*xm
        my=onehot(ys,H)
        xmb=xm.astype(jnp.bfloat16)
        one=jnp.where(my,jnp.bfloat16(1),jnp.bfloat16(0))
        oh=jnp.concatenate([one*jnp.where(xmb==m,jnp.bfloat16(1),jnp.bfloat16(0)) for m in range(4)],0)
        t=jnp.dot(tab_ref[:,:512],oh,preferred_element_type=jnp.float32)+jnp.dot(tab_ref[:,512:],oh,preferred_element_type=jnp.float32)
        mq=lax.broadcasted_iota(jnp.int32,(64,L),0).astype(jnp.float32)==xq
        for r in range(2):
            o=jnp.sum(jnp.where(mq,t[64*r:64*r+64,:],0.0),0,keepdims=True)
            for s in range(L//128):
                out_ref[c,s,r:r+1,:]=o[:,128*s:128*s+128]
        return 0
    lax.fori_loop(0,n_lists,pick,0,unroll=4)
def spatial(inp,interpret=False):
    bx,by,lam=constants()
    f=lambda a: jnp.asarray(a.astype(np.float32))
    L=inp.shape[2]
    vm=pl.BlockSpec(memory_space=pltpu.VMEM)
    return pl.pallas_call(spatial_kernel,
        out_shape=jax.ShapeDtypeStruct((inp.shape[0],L//128,2,128),jnp.float32),
        in_specs=[vm]*6,out_specs=vm,
        scratch_shapes=[pltpu.VMEM((768,256),jnp.float32),pltpu.VMEM((128,1024),jnp.bfloat16)],
        interpret=interpret,
        name="spatial",
    )(inp,f(bx.T),f(bx.T),f(by),f(by.T),f(lam))


CELL = ("z", "y_hi", "core")
PERIOD = ("x", "y_lo")


def group_sum(values, axes, count):
    spread = jnp.broadcast_to(values[None], (count,) + values.shape)
    return jnp.sum(lax.all_to_all(spread, axes, 0, 0, tiled=True), axis=0)


def on_device(footprints, cell_coords, obs_period, temporal_cov):
    obs_count, per_local, cell_local = footprints.shape
    cell_size, period_size = 32, 8
    period_first = lax.axis_index(PERIOD) * per_local
    period_ids = period_first + jnp.arange(per_local, dtype=jnp.int32)
    keep = (period_ids[None, :, None] <= obs_period[:, None, None]).astype(jnp.float32)
    masked = footprints * keep
    places = jnp.broadcast_to(cell_coords.astype(jnp.float32)[None], (obs_count, 2, cell_local))
    rows = lax.all_to_all(jnp.concatenate([masked, places], 1), CELL, 0, 0, tiled=True)
    mixed_cells = spatial(rows)
    by_cell = lax.all_to_all(
        mixed_cells.reshape(cell_size * period_size, per_local, 128), CELL + PERIOD, 0, 0, tiled=True
    )
    by_cell = by_cell.reshape(obs_count, period_size * per_local, 128)
    mixed = jnp.einsum("tu,nuj->tnj", temporal_cov, by_cell, precision=lax.Precision.HIGHEST)
    mixed = lax.all_to_all(
        mixed.reshape(period_size, per_local, obs_count, 128), PERIOD, 0, 0, tiled=True
    )
    hq_field = jnp.transpose(mixed, (2, 1, 0, 3)).reshape(obs_count, per_local, cell_local)
    gram = jnp.einsum("ntj,mtj->nm", hq_field, masked, precision=lax.Precision.HIGHEST)
    gram = group_sum(gram.reshape(obs_count * obs_count), ("x", "y_lo", "core"), 16)
    gram = group_sum(gram, ("z", "y_hi"), 16)
    return (hq_field, gram.reshape(obs_count, obs_count))


def solution(mesh):
    fine = Mesh(mesh.devices.reshape(8, 2, 2, 4, 2), CELL + PERIOD)
    return jax.shard_map(
        on_device,
        mesh=fine,
        in_specs=(P(None, PERIOD, CELL), P(None, CELL), P(), P()),
        out_specs=(P(None, PERIOD, CELL), P()),
        check_vma=False,
    )
```

```python
import jax
import jax.numpy as jnp
import numpy as np
from jax import lax
from jax.experimental import pallas as pl
from jax.experimental.pallas import tpu as pltpu
from jax.sharding import Mesh, PartitionSpec as P

LENGTH_SCALE = 48.0
WIDTH, HEIGHT = 256, 128
BF16, F32 = jnp.bfloat16, jnp.float32
ROWS_BY_ROWS = (((1,), (1,)), ((), ()))


def real_basis(size, keep):
    wave = np.arange(size)
    freq = np.where(wave <= size // 2, wave, size - wave)
    angle = 2 * np.pi * ((freq[:, None] * np.arange(keep)[None, :]) % size) / size
    basis = np.where(wave[:, None] <= size // 2, np.cos(angle), np.sin(angle)) * np.sqrt(2.0 / size)
    basis[0] /= np.sqrt(2.0)
    basis[size // 2] /= np.sqrt(2.0)
    return basis, freq


def constants():
    basis_x, freq_x = real_basis(2 * WIDTH, WIDTH)
    basis_y, freq_y = real_basis(2 * HEIGHT, HEIGHT)
    gap_x = np.minimum(np.arange(2 * WIDTH), 2 * WIDTH - np.arange(2 * WIDTH))
    gap_y = np.minimum(np.arange(2 * HEIGHT), 2 * HEIGHT - np.arange(2 * HEIGHT))
    tile = np.exp(-np.sqrt(gap_y[:, None] ** 2.0 + gap_x[None, :] ** 2.0) / LENGTH_SCALE)
    spectrum = np.real(np.fft.fft2(tile))[freq_y][:, freq_x]
    return basis_x, basis_y, spectrum


def host_pieces(values, count):
    pieces, rest = [], np.asarray(values, np.float64)
    for _ in range(count):
        piece = rest.astype(np.float32).astype(BF16)
        pieces.append(piece)
        rest = rest - piece.astype(np.float64)
    return pieces


def pieces_of(values, count):
    pieces = []
    for _ in range(count):
        piece = values.astype(BF16)
        pieces.append(piece)
        values = values - piece.astype(F32)
    return pieces


def product(a, b):
    return jnp.dot(a, b, preferred_element_type=F32)


def spatial_kernel(rows_ref, fx_ref, fy_ref, iy_ref, ix_ref, lam_ref, out_ref, acc_ref, table_ref):
    lists, _, length = rows_ref.shape
    acc_ref[...] = jnp.zeros_like(acc_ref)

    def one_hot(index, count):
        ids = lax.broadcasted_iota(jnp.int32, (count, length), 0).astype(F32).astype(BF16)
        return ids == index.astype(BF16)

    def place(c, _):
        block = rows_ref[c]
        in_row = one_hot(block[3:4, :], HEIGHT)
        in_column = jnp.where(one_hot(block[2:3, :], WIDTH), BF16(1), BF16(0))
        pieces = [pieces_of(block[r : r + 1, :], 3) for r in range(2)]
        spread = [jnp.where(in_row, pieces[r][s], BF16(0)) for s in range(3) for r in range(2)]
        acc_ref[...] += lax.dot_general(
            jnp.concatenate(spread, 0), in_column, ROWS_BY_ROWS, preferred_element_type=F32
        )
        return 0

    lax.fori_loop(0, lists, place, 0, unroll=8)

    grid = acc_ref[...].astype(BF16)
    p0 = product(grid, fx_ref[0])
    p1 = product(grid[:512], fx_ref[1])
    p2 = product(grid[:256], fx_ref[2])
    along_x = p0[:256] + ((p0[256:512] + p1[:256]) + (p0[512:] + p1[256:] + p2))
    u = [jnp.concatenate([part[:128], part[128:]], 1) for part in pieces_of(along_x, 3)]
    waves = product(fy_ref[0], jnp.concatenate([u[0], u[1]], 0)) + (
        product(fy_ref[1], jnp.concatenate([u[0], u[1]], 0))
        + product(fy_ref[2], jnp.concatenate([u[0], u[2]], 0))
    )
    waves = waves * jnp.concatenate([lam_ref[...]] * 2, 1)
    w = pieces_of(waves, 2)
    q = product(iy_ref[...], w[0])
    v = q[:128] + (q[128:] + product(iy_ref[:128], w[1]))
    v = pieces_of(jnp.concatenate([v[:, :512], v[:, 512:]], 0), 2)
    q = lax.dot_general(ix_ref[...], v[0], ROWS_BY_ROWS, preferred_element_type=F32)
    field = q[:256] + (
        q[256:] + lax.dot_general(ix_ref[:256], v[1], ROWS_BY_ROWS, preferred_element_type=F32)
    )
    for s, part in enumerate(pieces_of(field, 2)):
        for r in range(2):
            for m in range(2):
                table_ref[256 * s + 128 * r : 256 * s + 128 * r + 128, 128 * m : 128 * m + 128] = part[
                    128 * m : 128 * m + 128, 128 * r : 128 * r + 128
                ]

    def pick(c, _):
        block = rows_ref[c]
        xs = block[2:3, :]
        half = jnp.where(xs >= 128.0, 128.0, 0.0)
        hot = jnp.where(one_hot(block[3:4, :] + half, 256), BF16(1), BF16(0))
        found = product(table_ref[...], hot)
        in_column = lax.broadcasted_iota(jnp.int32, (128, length), 0).astype(F32) == xs - half
        for r in range(2):
            both = found[128 * r : 128 * r + 128] + found[256 + 128 * r : 384 + 128 * r]
            value = jnp.sum(jnp.where(in_column, both, 0.0), 0, keepdims=True)
            for s in range(length // 128):
                out_ref[c, s, r : r + 1, :] = value[:, 128 * s : 128 * s + 128]
        return 0

    lax.fori_loop(0, lists, pick, 0, unroll=8)


def spatial(rows):
    basis_x, basis_y, spectrum = constants()
    x, y = host_pieces(basis_x, 3), host_pieces(basis_y, 3)
    forward_x = np.stack([part.T for part in x])
    forward_y = np.stack([np.concatenate(pair, 1) for pair in ((y[0], y[1]), (y[1], y[0]), (y[2], y[0]))])
    inverse_y = np.concatenate([y[0].T, y[1].T], 0)
    inverse_x = np.concatenate([x[0].T, x[1].T], 0)
    whole = pl.BlockSpec(memory_space=pltpu.VMEM)
    lists, _, length = rows.shape
    return pl.pallas_call(
        spatial_kernel,
        out_shape=jax.ShapeDtypeStruct((lists, length // 128, 2, 128), F32),
        in_specs=[whole] * 6,
        out_specs=whole,
        scratch_shapes=[pltpu.VMEM((768, 256), F32), pltpu.VMEM((512, 256), BF16)],
        compiler_params=pltpu.CompilerParams(vmem_limit_bytes=24 * 1024 * 1024),
        name="spatial",
    )(rows, jnp.asarray(forward_x), jnp.asarray(forward_y), jnp.asarray(inverse_y), jnp.asarray(inverse_x),
      jnp.asarray(spectrum, F32))


CELL = ("z", "y_hi", "core")
PERIOD = ("x", "y_lo")


def group_sum(values, axes, count):
    spread = jnp.broadcast_to(values[None], (count,) + values.shape)
    return jnp.sum(lax.all_to_all(spread, axes, 0, 0, tiled=True), axis=0)


def on_device(footprints, cell_coords, obs_period, temporal_cov):
    obs_count, per_local, cell_local = footprints.shape
    cell_size, period_size = 32, 8
    period_first = lax.axis_index(PERIOD) * per_local
    period_ids = period_first + jnp.arange(per_local, dtype=jnp.int32)
    keep = (period_ids[None, :, None] <= obs_period[:, None, None]).astype(jnp.float32)
    masked = footprints * keep
    places = jnp.broadcast_to(cell_coords.astype(jnp.float32)[None], (obs_count, 2, cell_local))
    rows = lax.all_to_all(jnp.concatenate([masked, places], 1), CELL, 0, 0, tiled=True)
    mixed_cells = spatial(rows)
    by_cell = lax.all_to_all(
        mixed_cells.reshape(cell_size * period_size, per_local, 128), CELL + PERIOD, 0, 0, tiled=True
    )
    by_cell = by_cell.reshape(obs_count, period_size * per_local, 128)
    mixed = jnp.einsum("tu,nuj->tnj", temporal_cov, by_cell, precision=lax.Precision.HIGHEST)
    mixed = lax.all_to_all(
        mixed.reshape(period_size, per_local, obs_count, 128), PERIOD, 0, 0, tiled=True
    )
    hq_field = jnp.transpose(mixed, (2, 1, 0, 3)).reshape(obs_count, per_local, cell_local)
    gram = jnp.einsum("ntj,mtj->nm", hq_field, masked, precision=lax.Precision.HIGHEST)
    gram = group_sum(gram.reshape(obs_count * obs_count), ("x", "y_lo", "core"), 16)
    gram = group_sum(gram, ("z", "y_hi"), 16)
    return (hq_field, gram.reshape(obs_count, obs_count))


def solution(mesh):
    fine = Mesh(mesh.devices.reshape(8, 2, 2, 4, 2), CELL + PERIOD)
    return jax.shard_map(
        on_device,
        mesh=fine,
        in_specs=(P(None, PERIOD, CELL), P(None, CELL), P(), P()),
        out_specs=(P(None, PERIOD, CELL), P()),
        check_vma=False,
    )
```

```python
import jax
import jax.numpy as jnp
import numpy as np
from jax import lax
from jax.experimental import pallas as pl
from jax.experimental.pallas import tpu as pltpu
from jax.sharding import Mesh, PartitionSpec as P

LENGTH_SCALE = 48.0
WIDTH, HEIGHT = 256, 128
BF16, F32 = jnp.bfloat16, jnp.float32
ROWS_BY_ROWS = (((1,), (1,)), ((), ()))


def real_basis(size, keep):
    wave = np.arange(size)
    freq = np.where(wave <= size // 2, wave, size - wave)
    angle = 2 * np.pi * ((freq[:, None] * np.arange(keep)[None, :]) % size) / size
    basis = np.where(wave[:, None] <= size // 2, np.cos(angle), np.sin(angle)) * np.sqrt(2.0 / size)
    basis[0] /= np.sqrt(2.0)
    basis[size // 2] /= np.sqrt(2.0)
    return basis, freq


def constants():
    basis_x, freq_x = real_basis(2 * WIDTH, WIDTH)
    basis_y, freq_y = real_basis(2 * HEIGHT, HEIGHT)
    gap_x = np.minimum(np.arange(2 * WIDTH), 2 * WIDTH - np.arange(2 * WIDTH))
    gap_y = np.minimum(np.arange(2 * HEIGHT), 2 * HEIGHT - np.arange(2 * HEIGHT))
    tile = np.exp(-np.sqrt(gap_y[:, None] ** 2.0 + gap_x[None, :] ** 2.0) / LENGTH_SCALE)
    spectrum = np.real(np.fft.fft2(tile))[freq_y][:, freq_x]
    return basis_x, basis_y, spectrum


def host_pieces(values, count):
    pieces, rest = [], np.asarray(values, np.float64)
    for _ in range(count):
        piece = rest.astype(np.float32).astype(BF16)
        pieces.append(piece)
        rest = rest - piece.astype(np.float64)
    return pieces


def pieces_of(values, count):
    pieces = []
    for _ in range(count):
        piece = values.astype(BF16)
        pieces.append(piece)
        values = values - piece.astype(F32)
    return pieces


def product(a, b):
    return jnp.dot(a, b, preferred_element_type=F32)


def spatial_kernel(rows_ref, fx_ref, fy_ref, iy_ref, ix_ref, lam_ref, out_ref, acc_ref, table_ref):
    lists, _, length = rows_ref.shape
    acc_ref[...] = jnp.zeros_like(acc_ref)

    def one_hot(index, count):
        ids = lax.broadcasted_iota(jnp.int32, (count, length), 0).astype(F32).astype(BF16)
        return ids == index.astype(BF16)

    def place(c, _):
        block = rows_ref[c]
        in_row = one_hot(block[3:4, :], HEIGHT)
        in_column = jnp.where(one_hot(block[2:3, :], WIDTH), BF16(1), BF16(0))
        pieces = [pieces_of(block[r : r + 1, :], 3) for r in range(2)]
        spread = [jnp.where(in_row, pieces[r][s], BF16(0)) for s in range(3) for r in range(2)]
        acc_ref[...] += lax.dot_general(
            jnp.concatenate(spread, 0), in_column, ROWS_BY_ROWS, preferred_element_type=F32
        )
        return 0

    lax.fori_loop(0, lists, place, 0, unroll=8)

    grid = acc_ref[...].astype(BF16)
    p0 = product(grid, fx_ref[0])
    p1 = product(grid[:512], fx_ref[1])
    p2 = product(grid[:256], fx_ref[2])
    along_x = p0[:256] + ((p0[256:512] + p1[:256]) + (p0[512:] + p1[256:] + p2))
    u = [jnp.concatenate([part[:128], part[128:]], 1) for part in pieces_of(along_x, 3)]
    waves = product(fy_ref[0], jnp.concatenate([u[0], u[1]], 0)) + (
        product(fy_ref[1], jnp.concatenate([u[0], u[1]], 0))
        + product(fy_ref[2], jnp.concatenate([u[0], u[2]], 0))
    )
    waves = waves * jnp.concatenate([lam_ref[...]] * 2, 1)
    w = pieces_of(waves, 2)
    q = product(iy_ref[...], w[0])
    v = q[:128] + (q[128:] + product(iy_ref[:128], w[1]))
    v = pieces_of(jnp.concatenate([v[:, :512], v[:, 512:]], 0), 2)
    q = lax.dot_general(ix_ref[...], v[0], ROWS_BY_ROWS, preferred_element_type=F32)
    field = q[:256] + (
        q[256:] + lax.dot_general(ix_ref[:256], v[1], ROWS_BY_ROWS, preferred_element_type=F32)
    )
    for s, part in enumerate(pieces_of(field, 2)):
        for r in range(2):
            for m in range(2):
                table_ref[256 * s + 128 * r : 256 * s + 128 * r + 128, 128 * m : 128 * m + 128] = part[
                    128 * m : 128 * m + 128, 128 * r : 128 * r + 128
                ]

    def pick(c, _):
        block = rows_ref[c]
        xs = block[2:3, :]
        half = jnp.where(xs >= 128.0, 128.0, 0.0)
        hot = jnp.where(one_hot(block[3:4, :] + half, 256), BF16(1), BF16(0))
        found = product(table_ref[...], hot)
        in_column = lax.broadcasted_iota(jnp.int32, (128, length), 0).astype(F32) == xs - half
        for r in range(2):
            both = found[128 * r : 128 * r + 128] + found[256 + 128 * r : 384 + 128 * r]
            value = jnp.sum(jnp.where(in_column, both, 0.0), 0, keepdims=True)
            for s in range(length // 128):
                out_ref[c, s, r : r + 1, :] = value[:, 128 * s : 128 * s + 128]
        return 0

    lax.fori_loop(0, lists, pick, 0, unroll=8)


def spatial(rows):
    basis_x, basis_y, spectrum = constants()
    x, y = host_pieces(basis_x, 3), host_pieces(basis_y, 3)
    forward_x = np.stack([part.T for part in x])
    forward_y = np.stack([np.concatenate(pair, 1) for pair in ((y[0], y[1]), (y[1], y[0]), (y[2], y[0]))])
    inverse_y = np.concatenate([y[0].T, y[1].T], 0)
    inverse_x = np.concatenate([x[0].T, x[1].T], 0)
    whole = pl.BlockSpec(memory_space=pltpu.VMEM)
    lists, _, length = rows.shape
    return pl.pallas_call(
        spatial_kernel,
        out_shape=jax.ShapeDtypeStruct((lists, length // 128, 2, 128), F32),
        in_specs=[whole] * 6,
        out_specs=whole,
        scratch_shapes=[pltpu.VMEM((768, 256), F32), pltpu.VMEM((512, 256), BF16)],
        compiler_params=pltpu.CompilerParams(vmem_limit_bytes=24 * 1024 * 1024),
        name="spatial",
    )(rows, jnp.asarray(forward_x), jnp.asarray(forward_y), jnp.asarray(inverse_y), jnp.asarray(inverse_x),
      jnp.asarray(spectrum, F32))


CELL = ("z", "y_hi", "core")
PERIOD = ("x", "y_lo")


def group_sum(values, axes, count):
    spread = jnp.broadcast_to(values[None], (count,) + values.shape)
    return jnp.sum(lax.all_to_all(spread, axes, 0, 0, tiled=True), axis=0)


def on_device(footprints, cell_coords, obs_period, temporal_cov):
    obs_count, per_local, cell_local = footprints.shape
    cell_size, period_size = 32, 8
    period_first = lax.axis_index(PERIOD) * per_local
    period_ids = period_first + jnp.arange(per_local, dtype=jnp.int32)
    keep = (period_ids[None, :, None] <= obs_period[:, None, None]).astype(jnp.float32)
    masked = footprints * keep
    places = jnp.broadcast_to(cell_coords.astype(jnp.float32)[None], (obs_count, 2, cell_local))
    rows = lax.all_to_all(jnp.concatenate([masked, places], 1), CELL, 0, 0, tiled=True)
    mixed_cells = spatial(rows)
    by_cell = lax.all_to_all(
        mixed_cells.reshape(cell_size * period_size, per_local, 128), CELL + PERIOD, 0, 0, tiled=True
    )
    by_cell = by_cell.reshape(obs_count, period_size * per_local, 128)
    mixed = jnp.einsum("tu,nuj->tnj", temporal_cov, by_cell, precision=lax.Precision.HIGHEST)
    mixed = lax.all_to_all(
        mixed.reshape(period_size, per_local, obs_count, 128), PERIOD, 0, 0, tiled=True
    )
    hq_field = jnp.transpose(mixed, (2, 1, 0, 3)).reshape(obs_count, per_local, cell_local)
    gram = jnp.einsum("ntj,mtj->nm", hq_field, masked, precision=lax.Precision.HIGHEST)
    gram = group_sum(gram.reshape(obs_count * obs_count), ("y_hi", "core", "x", "y_lo"), 32)
    gram = group_sum(gram, ("z",), 8)
    return (hq_field, gram.reshape(obs_count, obs_count))


def solution(mesh):
    fine = Mesh(mesh.devices.reshape(8, 2, 2, 4, 2), CELL + PERIOD)
    return jax.shard_map(
        on_device,
        mesh=fine,
        in_specs=(P(None, PERIOD, CELL), P(None, CELL), P(), P()),
        out_specs=(P(None, PERIOD, CELL), P()),
        check_vma=False,
    )
```

```python
import jax
import jax.numpy as jnp
import numpy as np
from jax import lax
from jax.experimental import pallas as pl
from jax.experimental.pallas import tpu as pltpu
from jax.sharding import Mesh, PartitionSpec as P

LENGTH_SCALE = 48.0
WIDTH, HEIGHT = 256, 128
BF16, F32 = jnp.bfloat16, jnp.float32
ROWS_BY_ROWS = (((1,), (1,)), ((), ()))


def real_basis(size, keep):
    wave = np.arange(size)
    freq = np.where(wave <= size // 2, wave, size - wave)
    angle = 2 * np.pi * ((freq[:, None] * np.arange(keep)[None, :]) % size) / size
    basis = np.where(wave[:, None] <= size // 2, np.cos(angle), np.sin(angle)) * np.sqrt(2.0 / size)
    basis[0] /= np.sqrt(2.0)
    basis[size // 2] /= np.sqrt(2.0)
    return basis, freq


def constants():
    basis_x, freq_x = real_basis(2 * WIDTH, WIDTH)
    basis_y, freq_y = real_basis(2 * HEIGHT, HEIGHT)
    gap_x = np.minimum(np.arange(2 * WIDTH), 2 * WIDTH - np.arange(2 * WIDTH))
    gap_y = np.minimum(np.arange(2 * HEIGHT), 2 * HEIGHT - np.arange(2 * HEIGHT))
    tile = np.exp(-np.sqrt(gap_y[:, None] ** 2.0 + gap_x[None, :] ** 2.0) / LENGTH_SCALE)
    spectrum = np.real(np.fft.fft2(tile))[freq_y][:, freq_x]
    return basis_x, basis_y, spectrum


def host_pieces(values, count):
    pieces, rest = [], np.asarray(values, np.float64)
    for _ in range(count):
        piece = rest.astype(np.float32).astype(BF16)
        pieces.append(piece)
        rest = rest - piece.astype(np.float64)
    return pieces


def pieces_of(values, count):
    pieces = []
    for _ in range(count):
        piece = values.astype(BF16)
        pieces.append(piece)
        values = values - piece.astype(F32)
    return pieces


def product(a, b):
    return jnp.dot(a, b, preferred_element_type=F32)


def spatial_kernel(rows_ref, fx_ref, fy_ref, iy_ref, lam_ref, out_ref, acc_ref, table_ref):
    lists, _, length = rows_ref.shape
    acc_ref[...] = jnp.zeros_like(acc_ref)

    def one_hot(index, count):
        ids = lax.broadcasted_iota(jnp.int32, (count, length), 0).astype(F32).astype(BF16)
        return ids == index.astype(BF16)

    def place(c, _):
        block = rows_ref[c]
        in_row = one_hot(block[3:4, :], HEIGHT)
        in_column = jnp.where(one_hot(block[2:3, :], WIDTH), BF16(1), BF16(0))
        pieces = [pieces_of(block[r : r + 1, :], 3) for r in range(2)]
        spread = [jnp.where(in_row, pieces[r][s], BF16(0)) for s in range(3) for r in range(2)]
        acc_ref[...] += lax.dot_general(
            jnp.concatenate(spread, 0), in_column, ROWS_BY_ROWS, preferred_element_type=F32
        )
        return 0

    lax.fori_loop(0, lists, place, 0, unroll=16)

    grid = acc_ref[...].astype(BF16)
    p0 = product(grid, fx_ref[0])
    p1 = product(grid[:512], fx_ref[1])
    p2 = product(grid[:256], fx_ref[2])
    along_x = p0[:256] + ((p0[256:512] + p1[:256]) + (p0[512:] + p1[256:] + p2))
    u = [jnp.concatenate([part[:128], part[128:]], 1) for part in pieces_of(along_x, 3)]
    waves = product(fy_ref[0], jnp.concatenate([u[0], u[1]], 0)) + (
        product(fy_ref[1], jnp.concatenate([u[0], u[1]], 0))
        + product(fy_ref[2], jnp.concatenate([u[0], u[2]], 0))
    )
    waves = waves * jnp.concatenate([lam_ref[...]] * 2, 1)
    w = pieces_of(waves, 2)
    q = product(iy_ref[...], w[0])
    v = q[:128] + (q[128:] + product(iy_ref[:128], w[1]))
    v = pieces_of(jnp.concatenate([v[:, :512], v[:, 512:]], 0), 2)
    inverse_x = fx_ref[:2].reshape(2 * WIDTH, 2 * WIDTH)
    q = lax.dot_general(inverse_x, v[0], ROWS_BY_ROWS, preferred_element_type=F32)
    field = q[:256] + (
        q[256:] + lax.dot_general(fx_ref[0], v[1], ROWS_BY_ROWS, preferred_element_type=F32)
    )
    for s, part in enumerate(pieces_of(field, 2)):
        for r in range(2):
            for m in range(2):
                table_ref[256 * s + 128 * r : 256 * s + 128 * r + 128, 128 * m : 128 * m + 128] = part[
                    128 * m : 128 * m + 128, 128 * r : 128 * r + 128
                ]

    def pick(c, _):
        block = rows_ref[c]
        xs = block[2:3, :]
        half = jnp.where(xs >= 128.0, 128.0, 0.0)
        hot = jnp.where(one_hot(block[3:4, :] + half, 256), BF16(1), BF16(0))
        found = product(table_ref[...], hot)
        in_column = lax.broadcasted_iota(jnp.int32, (128, length), 0).astype(F32) == xs - half
        for r in range(2):
            both = found[128 * r : 128 * r + 128] + found[256 + 128 * r : 384 + 128 * r]
            value = jnp.sum(jnp.where(in_column, both, 0.0), 0, keepdims=True)
            for s in range(length // 128):
                out_ref[c, s, r : r + 1, :] = value[:, 128 * s : 128 * s + 128]
        return 0

    lax.fori_loop(0, lists, pick, 0, unroll=16)


def spatial(rows):
    basis_x, basis_y, spectrum = constants()
    x, y = host_pieces(basis_x, 3), host_pieces(basis_y, 3)
    forward_x = np.stack([part.T for part in x])
    forward_y = np.stack([np.concatenate(pair, 1) for pair in ((y[0], y[1]), (y[1], y[0]), (y[2], y[0]))])
    inverse_y = np.concatenate([y[0].T, y[1].T], 0)
    whole = pl.BlockSpec(memory_space=pltpu.VMEM)
    lists, _, length = rows.shape
    return pl.pallas_call(
        spatial_kernel,
        out_shape=jax.ShapeDtypeStruct((lists, length // 128, 2, 128), F32),
        in_specs=[whole] * 5,
        out_specs=whole,
        scratch_shapes=[pltpu.VMEM((768, 256), F32), pltpu.VMEM((512, 256), BF16)],
        compiler_params=pltpu.CompilerParams(vmem_limit_bytes=24 * 1024 * 1024),
        name="spatial",
    )(rows, jnp.asarray(forward_x), jnp.asarray(forward_y), jnp.asarray(inverse_y),
      jnp.asarray(spectrum, F32))


CELL = ("z", "y_hi", "core")
PERIOD = ("x", "y_lo")


def group_sum(values, axes, count):
    spread = jnp.broadcast_to(values[None], (count,) + values.shape)
    return jnp.sum(lax.all_to_all(spread, axes, 0, 0, tiled=True), axis=0)


def on_device(footprints, cell_coords, obs_period, temporal_cov):
    obs_count, per_local, cell_local = footprints.shape
    cell_size, period_size = 32, 8
    period_first = lax.axis_index(PERIOD) * per_local
    period_ids = period_first + jnp.arange(per_local, dtype=jnp.int32)
    keep = (period_ids[None, :, None] <= obs_period[:, None, None]).astype(jnp.float32)
    masked = footprints * keep
    places = jnp.broadcast_to(cell_coords.astype(jnp.float32)[None], (obs_count, 2, cell_local))
    rows = lax.all_to_all(jnp.concatenate([masked, places], 1), CELL, 0, 0, tiled=True)
    mixed_cells = spatial(rows)
    by_cell = lax.all_to_all(
        mixed_cells.reshape(cell_size * period_size, per_local, 128), CELL + PERIOD, 0, 0, tiled=True
    )
    by_cell = by_cell.reshape(obs_count, period_size * per_local, 128)
    mixed = jnp.einsum("tu,nuj->tnj", temporal_cov, by_cell, precision=lax.Precision.HIGHEST)
    mixed = lax.all_to_all(
        mixed.reshape(period_size, per_local, obs_count, 128), PERIOD, 0, 0, tiled=True
    )
    hq_field = jnp.transpose(mixed, (2, 1, 0, 3)).reshape(obs_count, per_local, cell_local)
    gram = jnp.einsum("ntj,mtj->nm", hq_field, masked, precision=lax.Precision.HIGHEST)
    gram = group_sum(gram.reshape(obs_count * obs_count), ("y_hi", "core", "x", "y_lo"), 32)
    gram = group_sum(gram, ("z",), 8)
    return (hq_field, gram.reshape(obs_count, obs_count))


def solution(mesh):
    fine = Mesh(mesh.devices.reshape(8, 2, 2, 4, 2), CELL + PERIOD)
    return jax.shard_map(
        on_device,
        mesh=fine,
        in_specs=(P(None, PERIOD, CELL), P(None, CELL), P(), P()),
        out_specs=(P(None, PERIOD, CELL), P()),
        check_vma=False,
    )
```
